32 devices in a mesh: row: 2 (over x), col: 16 (over z, y, core).
Axes of the slice: x: 2, y: 2, z: 4, core: 2. Of those that a mesh axis runs over, the one named last changes fastest.
Arguments:
- a_blocks: bfloat16 [512, 7, 64, 64], P(('row', 'col')), may hold values from -1.796875 to 1.796875
- p_blocks: bfloat16 [512, 64, 64], P(('row', 'col')), may hold values from -0.75 to 0.75
- a_peer: int32 [512, 7], P(('row', 'col')), may hold values from 0 to 15, all different within a row; in each aligned block of 16 rows (0 to 15, 16 to 31, ...) at most 8 rows name the same one
- a_local: int32 [512, 7], P(('row', 'col')), may hold values from 0 to 15
- agg_owner: int32 [512, 1], P(('row', 'col')), may hold values from 0 to 1; in each aligned block of 16 rows (0 to 15, 16 to 31, ...) at most 9 rows name the same one
- agg_local: int32 [512], P(('row', 'col')), may hold values from 0 to 3
- entry_slot: int32 [512, 7], P(('row', 'col')), may hold values from 0 to 6
Outputs:
- coarse: bfloat16 [128, 7, 64, 64], P(('row', 'col'))
The draws below stay inside these ranges and needn't reach their ends.
Inputs may be any that keep to these rules, and one draw needn't show every extreme that they name: `a_peer`: each fine block row names 7 different devices; among the rows of one device no device is named more than 8 times, and some device is named exactly that often. `agg_owner`: among the rows of one device no region is named more than 9 times, and some region is named exactly that often.
All inputs are finite; a program needn't handle non-finite values.
Results may differ from the reference program's by a relative error of at most 0.0049.
Values may be sent and summed in bfloat16 or wider, within the bound.
No kernel may reach another device: no remote copies, remote signals or barrier semaphores. Data moves between devices by JAX's collectives and lax.ppermute only.
A program may use at most 64 MiB of HBM per device.

```python
import math
import jax
import jax.numpy as jnp
import numpy as np
from jax import lax

B = 64
FB_DEV = 16
KA = 7
KC = 7
NC_DEV = 4
N = 512
NC = 128
CAPQ = 8
CAP = 9
N_ROW = 2
N_COL = 16


def plant(entries, own_key, low, high):
    place = [jax.random.randint(jax.random.fold_in(own_key, axis), (), 0, length) for axis, length in enumerate(entries.shape)]
    widest = entries.shape.index(max(entries.shape))
    neighbour = place[:widest] + [(place[widest] + 1) % entries.shape[widest]] + place[widest + 1:]
    return entries.at[tuple(place)].set(low).at[tuple(neighbour)].set(high)


def shard_levels(own_key, shape, split, low, largest):
    def one(dim, parts):
        heights = jax.random.uniform(jax.random.fold_in(jax.random.fold_in(own_key, 6), dim), (parts,), jnp.float32, low / len(split), largest / len(split))
        return jnp.repeat(jnp.exp(heights), shape[dim] // parts).reshape((-1,) + (1,) * (len(shape) - dim - 1))

    factor_of = one(*split[0])
    for cut in split[1:]:
        factor_of = factor_of * one(*cut)
    return factor_of


def deal_out(stream_key, own, number, rows, number_of, top, most, skew):
    order = jax.random.permutation(stream_key, number_of)
    crowded, common = load_shares(number_of, rows * top, most, skew, True), load_shares(number_of, rows * top, most, skew, False)
    places = jnp.arange(number_of)

    def named(tallies, turn):
        used = int((tallies > 0).sum())
        fixed = max(1, used // 4)
        moved = fixed + (places - fixed + turn * (used - fixed)) % max(1, number_of - fixed)
        return jnp.zeros((number_of,), jnp.int32).at[order[jnp.where(places < fixed, places, moved)]].set(jnp.asarray(tallies, jnp.int32))

    tallies = jnp.where(number % 4 == 0, named(crowded, number // 4), named(common, number - number // 4 - 1))
    mixed = jax.random.permutation(jax.random.fold_in(own, 3), number_of)
    donor, sink = mixed[0:number_of // 2 * 2:2], mixed[1:number_of // 2 * 2:2]
    room = jnp.minimum(tallies[donor] - 1, most - tallies[sink]) // 2
    room = jnp.where((donor == order[0]) | (sink == order[0]) | (tallies[sink] == 0), 0, jnp.maximum(room, 0))
    moved = jax.random.randint(jax.random.fold_in(own, 4), (number_of // 2,), 0, 1 << 20) % (room + 1)
    tallies = tallies.at[donor].add(-moved).at[sink].add(moved)
    labels = jnp.searchsorted(jnp.cumsum(tallies), jnp.arange(rows * top), side="right").astype(jnp.int32)
    grid = labels.reshape(top, rows).T
    grid = grid[jax.random.permutation(jax.random.fold_in(own, 1), rows)]
    turn = jax.random.randint(jax.random.fold_in(own, 2), (rows, 1), 0, top)
    return jnp.take_along_axis(grid, (jnp.arange(top)[None, :] + turn) % top, axis=1)


def load_shares(count, total, most, skew, full):
    weights = [(1 << 20) // math.isqrt(rank ** skew) + 1 for rank in range(1, count + 1)]
    largest = most if full else min(most, max(-(-total // count), total * weights[0] // sum(weights)))
    least = 1 if total - largest >= count - 1 else 0
    holding, rest = [largest] + [least] * (count - 1), total - largest - least * (count - 1)
    while rest > 0:
        free = [i for i in range(1, count) if holding[i] < largest] or [i for i in range(1, count) if holding[i] < most]
        pool, remaining = sum([weights[i] for i in free]), rest
        for i in free:
            more = min(most - holding[i], max(1, remaining * weights[i] // pool), rest)
            holding[i] = holding[i] + more
            rest = rest - more
    return np.array(holding)


def normal_values(rng, shape, width, reach, cuts=(), held_as=jnp.bfloat16):
    loudness = shard_levels(rng, shape, cuts, -0.22, 0.18) if cuts else 1.0
    drawn = jax.random.normal(rng, shape, jnp.float32) * width * loudness
    return jnp.minimum(jnp.maximum(drawn, -reach), reach).astype(held_as)


def setup_inputs(seed: int = 0) -> dict:
    arg_keys = jax.random.split(jax.random.key(seed), 8)
    a_blocks = normal_values(arg_keys[0], (N, KA, B, B), 0.3, 1.796875, ((0, 32),))
    p_blocks = normal_values(arg_keys[1], (N, B, B), B ** -0.5, 0.75, ((0, 32),))
    a_peer_keys = jax.random.split(jax.random.fold_in(arg_keys[2], 1), N // FB_DEV)
    a_peer_turns = jax.random.permutation(jax.random.fold_in(arg_keys[2], 3), N // FB_DEV)
    a_peer = jax.vmap(lambda own, number: deal_out(jax.random.fold_in(arg_keys[2], 2), own, number, FB_DEV, N_COL, KA, CAPQ, 2))(a_peer_keys, a_peer_turns).reshape((N, KA))
    a_local = plant(jax.random.randint(arg_keys[3], (N, KA), 0, FB_DEV), jax.random.fold_in(arg_keys[3], 1), 0, FB_DEV - 1).astype(jnp.int32)
    agg_owner_keys = jax.random.split(jax.random.fold_in(arg_keys[4], 1), N // FB_DEV)
    agg_owner_turns = jax.random.permutation(jax.random.fold_in(arg_keys[4], 3), N // FB_DEV)
    agg_owner = jax.vmap(lambda own, number: deal_out(jax.random.fold_in(arg_keys[4], 2), own, number, FB_DEV, N_ROW, 1, CAP, 1))(agg_owner_keys, agg_owner_turns).reshape((N, 1))
    agg_local = plant(jax.random.randint(arg_keys[5], (N,), 0, NC_DEV), jax.random.fold_in(arg_keys[5], 1), 0, NC_DEV - 1).astype(jnp.int32)
    entry_slot = plant(jax.random.randint(arg_keys[6], (N, KA), 0, KC), jax.random.fold_in(arg_keys[6], 1), 0, KC - 1).astype(jnp.int32)
    return dict(a_blocks=a_blocks, p_blocks=p_blocks, a_peer=a_peer, a_local=a_local, agg_owner=agg_owner, agg_local=agg_local, entry_slot=entry_slot)


def reference(a_blocks, p_blocks, a_peer, a_local, agg_owner, agg_local, entry_slot):
    region_len = FB_DEV * N_COL
    row_ids = jnp.arange(N, dtype=jnp.int32)
    columns = (row_ids // region_len * region_len)[:, None] + a_peer * FB_DEV + a_local
    coarse_row = (agg_owner[:, 0] * N_COL + (row_ids // FB_DEV) % N_COL) * NC_DEV + agg_local
    targets = coarse_row[:, None] * KC + entry_slot

    def one_region(current, region):
        first_row = (region * region_len).astype(jnp.int32)
        fine_part = lax.dynamic_slice_in_dim(a_blocks, first_row, region_len, 0)
        own_prolong = lax.dynamic_slice_in_dim(p_blocks, first_row, region_len, 0)
        region_cols = lax.dynamic_slice_in_dim(columns, first_row, region_len, 0)
        region_targets = lax.dynamic_slice_in_dim(targets, first_row, region_len, 0)
        fetched = p_blocks[region_cols]
        product_ap = jnp.einsum('nkab,nkbc->nkac', fine_part.astype(jnp.float32), fetched.astype(jnp.float32)).astype(jnp.bfloat16)
        terms = jnp.einsum('nba,nkbc->nkac', own_prolong.astype(jnp.float32), product_ap.astype(jnp.float32))
        summed = jax.ops.segment_sum(terms.reshape(-1, B * B), region_targets.reshape(-1), num_segments=NC * KC)
        return current + summed, None

    start_sum = jnp.zeros((NC * KC, B * B), jnp.float32)
    result_sum, _ = lax.scan(one_region, start_sum, jnp.arange(N_ROW, dtype=jnp.int32))
    return result_sum.reshape(NC, KC, B, B).astype(jnp.bfloat16)
```

```python
import jax
import jax.numpy as jnp
from jax import lax
from jax.experimental import pallas as pl
from jax.experimental.pallas import tpu as pltpu
from jax.sharding import PartitionSpec as P

KC = 7
NC_DEV = 4
VMEM = pl.BlockSpec(memory_space=pltpu.VMEM)
SMEM = pl.BlockSpec(memory_space=pltpu.SMEM)


def ring_position(index, chips):
    z, y = index // 4, index // 2 % 2
    return z + y * (chips - 1 - 2 * z)


def pack_kernel(p_ref, out_ref):
    pairs, order, _ = out_ref.shape
    for j in range(pairs):
        out_ref[j] = jnp.concatenate([p_ref[j], p_ref[j + pairs]], axis=1)


def left_kernel(a_ref, p_ref, x_ref):
    rows, entries = a_ref.shape[:2]
    for i in range(rows):
        for k in range(entries):
            x = lax.dot_general(
                p_ref[i], a_ref[i, k], (((0,), (0,)), ((), ())), preferred_element_type=jnp.float32
            )
            x_ref[i * entries + k] = x.astype(x_ref.dtype)


def fold(acc_ref, base, half, j, low):
    rows = acc_ref.shape[0] // 2
    first = jnp.where(low, acc_ref[base + j], acc_ref[rows + base + half + j])
    second = jnp.where(low, acc_ref[base + half + j], acc_ref[rows + base + j])
    order = first.shape[1] // 2
    return first + pltpu.roll(second, order, axis=1)


def sum_kernel(code_ref, x_ref, *refs):
    *pieces, own_ref, sent_ref, gathered_ref, acc_ref = refs
    entries, rows = code_ref.shape
    pairs, order, width = pieces[0].shape
    acc_ref[...] = jnp.zeros_like(acc_ref)
    for n, piece in enumerate(pieces):
        gathered_ref[n * pairs : (n + 1) * pairs] = piece[...]
    for i in range(rows):
        for k in range(entries):
            code = code_ref[k, i]
            source, target = code >> 16, code & 0xFFFF
            acc_ref[target] += jnp.dot(
                x_ref[i * entries + k], gathered_ref[source], preferred_element_type=jnp.float32
            )
    lanes = lax.broadcasted_iota(jnp.int32, (order, width), 1)
    low = lanes < width // 2
    half = own_ref.shape[0]
    for j in range(half):
        own_ref[j] = fold(acc_ref, 0, half, j, low)
    for n in range(sent_ref.shape[0]):
        for j in range(half):
            sent_ref[n, j] = fold(acc_ref, 2 * half * (n + 1), half, j, low).astype(sent_ref.dtype)


def add_kernel(own_ref, *refs):
    *received, out_ref = refs
    half, order, width = own_ref.shape
    for j in range(half):
        total = own_ref[j]
        for ref in received:
            total = total + ref[j].astype(jnp.float32)
        total = total.astype(out_ref.dtype)
        out_ref[j] = total[:, : width // 2]
        out_ref[half + j] = total[:, width // 2 :]


def local(a_blocks, p_blocks, a_peer, a_local, agg_owner, agg_local, entry_slot):
    rows, entries, order, _ = a_blocks.shape
    columns, regions = lax.axis_size("col"), lax.axis_size("row")
    chips = columns // 2
    pairs = rows // 2
    lanes = NC_DEV * KC

    def toward(index, step):
        place = (ring_position(index, chips) + step) % chips
        z, y = (place, 0) if place < chips // 2 else (chips - 1 - place, 1)
        return z * 4 + y * 2 + index % 2

    ring = [(i, toward(i, 1 - 2 * (i % 2))) for i in range(columns)]
    swap = [(i, i ^ 1) for i in range(columns)]

    own = pl.pallas_call(
        pack_kernel,
        out_shape=jax.ShapeDtypeStruct((pairs, order, 2 * order), p_blocks.dtype),
        in_specs=[VMEM], out_specs=VMEM, name="pack",
    )(p_blocks)

    first, second = own, lax.ppermute(own, "col", swap)
    behind, ahead = {0: (own, second)}, {}
    for step in range(1, chips // 2 + 1):
        first = lax.ppermute(first, "col", ring)
        if step < chips // 2:
            second = lax.ppermute(second, "col", ring)
            behind[step] = (first, second)
            ahead[step] = (lax.ppermute(second, "col", swap), lax.ppermute(first, "col", swap))
        else:
            ahead[step] = (first, lax.ppermute(first, "col", swap))
    pieces = []
    for distance in range(chips):
        if distance == 0:
            pieces += behind[0]
        elif distance <= chips // 2:
            pieces += ahead[distance]
        else:
            pieces += behind[chips - distance]

    x = pl.pallas_call(
        left_kernel,
        out_shape=jax.ShapeDtypeStruct((rows * entries, order, order), jnp.bfloat16),
        in_specs=[VMEM, VMEM], out_specs=VMEM, name="left",
    )(a_blocks, p_blocks)

    me, region = lax.axis_index("col"), lax.axis_index("row")
    peer, place = a_peer.T, a_local.T
    turned = me % 2
    distance = ring_position(peer, chips) - ring_position(me, chips)
    distance = (distance * (1 - 2 * turned)) % chips
    source = (distance * 2 + (peer % 2) ^ turned) * pairs + place % pairs
    relative = (agg_owner.T - region) % regions
    target = relative * lanes + agg_local[None, :] * KC + entry_slot.T
    code = source * 65536 + target + (place // pairs) * (regions * lanes)

    half = lanes // 2
    width = 2 * order
    own_sum, sent = pl.pallas_call(
        sum_kernel,
        out_shape=(
            jax.ShapeDtypeStruct((half, order, width), jnp.float32),
            jax.ShapeDtypeStruct((regions - 1, half, order, width), jnp.bfloat16),
        ),
        in_specs=[SMEM] + [VMEM] * (1 + len(pieces)), out_specs=(VMEM, VMEM),
        scratch_shapes=[
            pltpu.VMEM((columns * pairs, order, width), p_blocks.dtype),
            pltpu.VMEM((2 * regions * lanes, order, width), jnp.float32),
        ],
        name="sum",
    )(code, x, *pieces)

    received = [
        lax.ppermute(sent[n - 1], "row", [(i, (i + n) % regions) for i in range(regions)])
        for n in range(1, regions)
    ]
    out = pl.pallas_call(
        add_kernel,
        out_shape=jax.ShapeDtypeStruct((lanes, order, order), jnp.bfloat16),
        in_specs=[VMEM] * regions, out_specs=VMEM, name="add",
    )(own_sum, *received)
    return out.reshape(NC_DEV, KC, order, order)


def solution(mesh):
    in_specs = (
        P(("row", "col"), None, None, None),
        P(("row", "col"), None, None),
        P(("row", "col"), None),
        P(("row", "col"), None),
        P(("row", "col"), None),
        P(("row", "col")),
        P(("row", "col"), None),
    )
    out_specs = P(("row", "col"), None, None, None)
    return jax.shard_map(local, mesh=mesh, in_specs=in_specs, out_specs=out_specs, check_vma=False)
```

```python
import jax
import jax.numpy as jnp
from jax import lax
from jax.experimental import pallas as pl
from jax.experimental.pallas import tpu as pltpu
from jax.sharding import PartitionSpec as P

KC = 7
NC_DEV = 4
VMEM = pl.BlockSpec(memory_space=pltpu.VMEM)
SMEM = pl.BlockSpec(memory_space=pltpu.SMEM)
HBM = pl.BlockSpec(memory_space=pltpu.HBM)
LIMIT = 1 << 20
PARTS = 8


def keep(*arrays):
    return [pltpu.with_memory_space_constraint(array, pltpu.VMEM) for array in arrays]


def routes(columns):
    near = {4: 0, 12: 0, 2: 0, 6: 4, 10: 2, 8: 12, 14: 12}
    order = [key for key in near if key < columns]
    far = list(range(16, columns, 2))
    parents = {key: near[key] for key in order} | {key: key & 15 for key in far}
    groups = [[0, 2, 4, 12], [10, 6], [8, 14], far]
    groups = [[key for key in group if key < columns] for group in groups]
    return order + far, parents, [group for group in groups if group]


def slots(columns):
    keys = [key ^ core for group in routes(columns)[2] for core in range(2) for key in group]
    return {key: slot for slot, key in enumerate(keys)}


def pack_kernel(p_ref, out_ref, kept_ref):
    pairs, _, _ = out_ref.shape
    kept_ref[...] = p_ref[...]
    for j in range(pairs):
        out_ref[j] = jnp.concatenate([p_ref[j], p_ref[j + pairs]], axis=1)


def merge_kernel(*refs):
    *pieces, out_ref = refs
    start = 0
    for piece in pieces:
        out_ref[start : start + piece.shape[0]] = piece[...]
        start += piece.shape[0]


def codes(peer_ref, place_ref, owner_ref, slot_ref, row_ref):
    rows = peer_ref.shape[1]
    columns, regions = lax.axis_size("col"), lax.axis_size("row")
    pairs, lanes = rows // 2, NC_DEV * KC
    me, region = lax.axis_index("col"), lax.axis_index("row")
    key, place = peer_ref[...] ^ me, place_ref[...]
    piece = jnp.zeros_like(key)
    for value, slot in slots(columns).items():
        piece = jnp.where(key == value, slot, piece)
    high = jnp.where(place < pairs, 0, 1)
    source = piece * pairs + place - high * pairs
    relative = owner_ref[...] - region
    relative = jnp.where(relative < 0, relative + regions, relative)
    target = (relative * NC_DEV + row_ref[...]) * KC + slot_ref[...]
    return source * 65536 + target + high * (regions * lanes)


def left_kernel(p_ref, a_ref, peer_ref, place_ref, owner_ref, slot_ref, row_ref, x_ref, out_ref, *held):
    *index_held, a_held, code_ref, index_sems, sems, code_sem = held
    rows, entries = a_ref.shape[:2]
    parts = sems.shape[0]
    step = rows // parts
    index_copies = [
        pltpu.make_async_copy(source, target, index_sems.at[n])
        for n, (source, target) in enumerate(
            zip((peer_ref, place_ref, owner_ref, slot_ref, row_ref), index_held)
        )
    ]
    for copy in index_copies:
        copy.start()
    copies = []
    for n in range(parts):
        part = pl.ds(n * step, step)
        copies.append(pltpu.make_async_copy(a_ref.at[part], a_held.at[part], sems.at[n]))
        copies[n].start()
    for copy in index_copies:
        copy.wait()
    code_ref[...] = codes(*index_held)
    code_copy = pltpu.make_async_copy(code_ref, out_ref, code_sem)
    code_copy.start()
    for n in range(parts):
        copies[n].wait()
        for i in range(n * step, (n + 1) * step):
            for k in range(entries):
                x = lax.dot_general(
                    p_ref[i], a_held[i, k], (((0,), (0,)), ((), ())),
                    preferred_element_type=jnp.float32,
                )
                x_ref[i * entries + k] = x.astype(x_ref.dtype)
    code_copy.wait()


def fold(acc_ref, base, half, j, low):
    rows = acc_ref.shape[0] // 2
    first = jnp.where(low, acc_ref[base + j], acc_ref[rows + base + half + j])
    second = jnp.where(low, acc_ref[base + half + j], acc_ref[rows + base + j])
    order = first.shape[1] // 2
    return first + pltpu.roll(second, order, axis=1)


def sum_kernel(code_ref, x_ref, *refs):
    *pieces, own_ref, sent_ref, gathered_ref, acc_ref = refs
    entries, rows = code_ref.shape
    order, width = pieces[0].shape[1:]
    acc_ref[...] = jnp.zeros_like(acc_ref)
    merge_kernel(*pieces, gathered_ref)
    for i in range(rows):
        for k in range(entries):
            code = code_ref[k, i]
            source, target = code >> 16, code & 0xFFFF
            acc_ref[target] += jnp.dot(
                x_ref[i * entries + k], gathered_ref[source], preferred_element_type=jnp.float32
            )
    lanes = lax.broadcasted_iota(jnp.int32, (order, width), 1)
    low = lanes < width // 2
    half = own_ref.shape[0]
    for j in range(half):
        own_ref[j] = fold(acc_ref, 0, half, j, low)
    for n in range(sent_ref.shape[0]):
        for j in range(half):
            sent_ref[n, j] = fold(acc_ref, 2 * half * (n + 1), half, j, low).astype(sent_ref.dtype)


def add_kernel(own_ref, *refs):
    *received, out_ref = refs
    half, _, width = own_ref.shape
    for j in range(half):
        total = own_ref[j]
        for ref in received:
            total = total + ref[j].astype(jnp.float32)
        out_ref[j] = total[:, : width // 2].astype(out_ref.dtype)
        out_ref[half + j] = pltpu.roll(total, width // 2, axis=1)[:, : width // 2].astype(out_ref.dtype)


def call(kernel, out_shape, in_specs, out_specs, scratch_shapes=(), limit=LIMIT):
    return pl.pallas_call(
        kernel, out_shape=out_shape, in_specs=in_specs, out_specs=out_specs,
        scratch_shapes=scratch_shapes,
        compiler_params=pltpu.CompilerParams(vmem_limit_bytes=limit),
    )


def local(a_blocks, p_blocks, a_peer, a_local, agg_owner, agg_local, entry_slot):
    rows, entries, order, _ = a_blocks.shape
    columns, regions = lax.axis_size("col"), lax.axis_size("row")
    pairs = rows // 2
    lanes = NC_DEV * KC

    def exchange(array, bits):
        return lax.ppermute(array, "col", [(i, i ^ bits) for i in range(columns)])

    own, kept = call(
        pack_kernel,
        (
            pltpu.VMEM((pairs, order, 2 * order), p_blocks.dtype),
            pltpu.VMEM(p_blocks.shape, p_blocks.dtype),
        ),
        [VMEM], (VMEM, VMEM),
    )(*keep(p_blocks))

    order_of, parents, groups = routes(columns)
    held = {0: own}
    for key in order_of:
        held[key] = exchange(held[parents[key]], key ^ parents[key])
    pieces = []
    for group in groups:
        mine = call(
            merge_kernel, pltpu.VMEM((len(group) * pairs, order, 2 * order), own.dtype),
            [VMEM] * len(group), VMEM,
        )(*keep(*[held[key] for key in group]))
        pieces += [mine, exchange(mine, 1)]

    indices = (a_peer.T, a_local.T, agg_owner.T, entry_slot.T, agg_local[None])
    x, code = call(
        left_kernel,
        (
            pltpu.VMEM((rows * entries, order, order), jnp.bfloat16),
            pltpu.SMEM((entries, rows), jnp.int32),
        ),
        [VMEM] + [HBM] * 6, (VMEM, SMEM),
        [pltpu.VMEM(array.shape, array.dtype) for array in indices]
        + [
            pltpu.VMEM(a_blocks.shape, a_blocks.dtype), pltpu.VMEM((entries, rows), jnp.int32),
            pltpu.SemaphoreType.DMA((len(indices),)), pltpu.SemaphoreType.DMA((PARTS,)),
            pltpu.SemaphoreType.DMA(()),
        ],
        limit=a_blocks.size * 4 + LIMIT,
    )(*keep(kept), *[pltpu.with_memory_space_constraint(v, pltpu.HBM) for v in (a_blocks, *indices)])

    half = lanes // 2
    width = 2 * order
    scratch = (columns * pairs * 2 + 2 * regions * lanes * 4) * order * width
    own_sum, sent = call(
        sum_kernel,
        (
            pltpu.VMEM((half, order, width), jnp.float32),
            pltpu.VMEM((regions - 1, half, order, width), jnp.bfloat16),
        ),
        [SMEM] + [VMEM] * (1 + len(pieces)), (VMEM, VMEM),
        [
            pltpu.VMEM((columns * pairs, order, width), p_blocks.dtype),
            pltpu.VMEM((2 * regions * lanes, order, width), jnp.float32),
        ],
        limit=scratch + LIMIT,
    )(pltpu.with_memory_space_constraint(code, pltpu.SMEM), *keep(x, *pieces))

    received = [
        lax.ppermute(sent[n - 1], "row", [(i, (i + n) % regions) for i in range(regions)])
        for n in range(1, regions)
    ]
    out = call(
        add_kernel, jax.ShapeDtypeStruct((lanes, order, order), jnp.bfloat16),
        [VMEM] * regions, VMEM, limit=4 << 20,
    )(*keep(own_sum, *received))
    return out.reshape(NC_DEV, KC, order, order)


def solution(mesh):
    in_specs = (
        P(("row", "col"), None, None, None),
        P(("row", "col"), None, None),
        P(("row", "col"), None),
        P(("row", "col"), None),
        P(("row", "col"), None),
        P(("row", "col")),
        P(("row", "col"), None),
    )
    out_specs = P(("row", "col"), None, None, None)

    return jax.shard_map(local, mesh=mesh, in_specs=in_specs, out_specs=out_specs, check_vma=False)
```

```python
import functools

import jax
import jax.numpy as jnp
from jax import lax
from jax.experimental import pallas as pl
from jax.experimental.pallas import tpu as pltpu
from jax.sharding import PartitionSpec as P

KC = 7
NC_DEV = 4
VMEM = pl.BlockSpec(memory_space=pltpu.VMEM)
SMEM = pl.BlockSpec(memory_space=pltpu.SMEM)
HBM = pl.BlockSpec(memory_space=pltpu.HBM)
LIMIT = 1 << 20
PARTS = 2


def keep(*arrays):
    return [pltpu.with_memory_space_constraint(array, pltpu.VMEM) for array in arrays]


def routes(columns):
    near = {12: 0, 2: 0, 4: 0, 10: 2, 8: 12, 14: 12, 6: 4}
    order = [key for key in near if key < columns]
    far = list(range(16, columns, 2))
    parents = {key: near[key] for key in order} | {key: key & 15 for key in far}
    groups = [[0, 2, 4, 12], [10, 8, 14], [6], far]
    groups = [[key for key in group if key < columns] for group in groups]
    return order + far, parents, [group for group in groups if group]


def slots(columns):
    keys = [key ^ core for group in routes(columns)[2] for core in range(2) for key in group]
    return {key: slot for slot, key in enumerate(keys)}


def pack_kernel(p_ref, out_ref, kept_ref):
    pairs, _, _ = out_ref.shape
    kept_ref[...] = p_ref[...]
    for j in range(pairs):
        out_ref[j] = jnp.concatenate([p_ref[j], p_ref[j + pairs]], axis=1)


def merge_kernel(*refs):
    *pieces, out_ref = refs
    start = 0
    for piece in pieces:
        out_ref[start : start + piece.shape[0]] = piece[...]
        start += piece.shape[0]


def codes(peer_ref, place_ref, owner_ref, slot_ref, row_ref):
    rows = peer_ref.shape[1]
    columns, regions = lax.axis_size("col"), lax.axis_size("row")
    pairs, lanes = rows // 2, NC_DEV * KC
    me, region = lax.axis_index("col"), lax.axis_index("row")
    key, place = peer_ref[...] ^ me, place_ref[...]
    piece = jnp.zeros_like(key)
    for value, slot in slots(columns).items():
        piece = jnp.where(key == value, slot, piece)
    high = jnp.where(place < pairs, 0, 1)
    source = piece * pairs + place - high * pairs
    relative = owner_ref[...] - region
    relative = jnp.where(relative < 0, relative + regions, relative)
    target = (relative * NC_DEV + row_ref[...]) * KC + slot_ref[...]
    return source * 65536 + target + high * (regions * lanes)


def visits(owner_ref):
    region, rows = lax.axis_index("row"), owner_ref.shape[1]
    column = lax.broadcasted_iota(jnp.int32, (rows, rows), 1)
    row = lax.broadcasted_iota(jnp.int32, (rows, rows), 0)
    away = jnp.where(owner_ref[...] != region, 1, 0) + jnp.zeros((rows, rows), jnp.int32)
    mine = jnp.sum(jnp.where(column == row, away, 0), axis=1, keepdims=True)
    before = jnp.sum(jnp.where(column < row, away, 0), axis=1, keepdims=True)
    total = jnp.sum(away, axis=1, keepdims=True)
    number = lax.broadcasted_iota(jnp.int32, (rows, 1), 0)
    place = jnp.where(mine > 0, before, total + number - before)
    return jnp.sum(jnp.where(place == column, row, 0), axis=0, keepdims=True)


def code_kernel(*refs):
    sources, (out_ref, *held, code_ref, sems) = refs[:5], refs[5:]
    copies = [
        pltpu.make_async_copy(source, target, sems.at[n])
        for n, (source, target) in enumerate(zip(sources, held))
    ]
    for copy in copies:
        copy.start()
    for copy in copies:
        copy.wait()
    entries = held[0].shape[0]
    code_ref[:entries] = codes(*held)
    code_ref[entries:] = visits(held[2])
    pltpu.sync_copy(code_ref, out_ref)


def left_kernel(p_ref, a_ref, x_ref, a_held, sems):
    rows, entries = a_ref.shape[:2]
    parts = sems.shape[0]
    step = rows // parts
    copies = []
    for n in range(parts):
        part = pl.ds(n * step, step)
        copies.append(pltpu.make_async_copy(a_ref.at[part], a_held.at[part], sems.at[n]))
        copies[n].start()
    for n in range(parts):
        copies[n].wait()
        for i in range(n * step, (n + 1) * step):
            for k in range(entries):
                x = lax.dot_general(
                    p_ref[i], a_held[i, k], (((0,), (0,)), ((), ())),
                    preferred_element_type=jnp.float32,
                )
                x_ref[i * entries + k] = x.astype(x_ref.dtype)


def fold(acc_ref, base, half, j, low):
    rows = acc_ref.shape[0] // 2
    first = jnp.where(low, acc_ref[base + j], acc_ref[rows + base + half + j])
    second = jnp.where(low, acc_ref[base + half + j], acc_ref[rows + base + j])
    order = first.shape[1] // 2
    return first + pltpu.roll(second, order, axis=1)


def accumulate(visited, code_ref, x_ref, gathered_ref, acc_ref):
    entries = code_ref.shape[0] - 1
    for i in visited:
        row = code_ref[entries, i]
        for k in range(entries):
            code = code_ref[k, row]
            source, target = code >> 16, code & 0xFFFF
            acc_ref[target] += jnp.dot(
                x_ref[row * entries + k], gathered_ref[source], preferred_element_type=jnp.float32
            )


def lower_half(order, width):
    return lax.broadcasted_iota(jnp.int32, (order, width), 1) < width // 2


def ready_kernel(*refs):
    *pieces, acc_ref, gathered_ref = refs
    acc_ref[...] = jnp.zeros_like(acc_ref)
    merge_kernel(*pieces, gathered_ref)


def away_kernel(visits, code_ref, x_ref, acc_in_ref, gathered_in_ref, *refs):
    *pieces, sent_ref, acc_ref, gathered_ref = refs
    regions, half, order, width = sent_ref.shape
    start = gathered_ref.shape[0] - sum(piece.shape[0] for piece in pieces)
    merge_kernel(*pieces, gathered_ref.at[start:])
    accumulate(range(visits), code_ref, x_ref, gathered_ref, acc_ref)
    low = lower_half(order, width)
    for n in range(regions):
        for j in range(half):
            sent_ref[n, j] = fold(acc_ref, 2 * half * (n + 1), half, j, low).astype(sent_ref.dtype)


def home_kernel(visits, code_ref, x_ref, gathered_ref, acc_in_ref, own_ref, acc_ref):
    half, order, width = own_ref.shape
    rows = code_ref.shape[1]
    total = acc_ref.shape[0] // 2
    for n in range(2):
        acc_ref[n * total : n * total + 2 * half] = acc_in_ref[n * total : n * total + 2 * half]
    accumulate(range(visits, rows), code_ref, x_ref, gathered_ref, acc_ref)
    low = lower_half(order, width)
    for j in range(half):
        own_ref[j] = fold(acc_ref, 0, half, j, low)


def add_kernel(own_ref, *refs):
    *received, out_ref = refs
    half, _, width = own_ref.shape
    for j in range(half):
        total = own_ref[j]
        for ref in received:
            total = total + ref[j].astype(jnp.float32)
        out_ref[j] = total[:, : width // 2].astype(out_ref.dtype)
        out_ref[half + j] = pltpu.roll(total, width // 2, axis=1)[:, : width // 2].astype(out_ref.dtype)


def call(kernel, out_shape, in_specs, out_specs, scratch_shapes=(), limit=LIMIT, aliases=None):
    return pl.pallas_call(
        kernel, out_shape=out_shape, in_specs=in_specs, out_specs=out_specs,
        scratch_shapes=scratch_shapes, input_output_aliases=aliases or {},
        compiler_params=pltpu.CompilerParams(vmem_limit_bytes=limit),
    )


def local(a_blocks, p_blocks, a_peer, a_local, agg_owner, agg_local, entry_slot):
    rows, entries, order, _ = a_blocks.shape
    columns, regions = lax.axis_size("col"), lax.axis_size("row")
    pairs = rows // 2
    lanes = NC_DEV * KC

    def exchange(array, bits):
        return lax.ppermute(array, "col", [(i, i ^ bits) for i in range(columns)])

    own, kept = call(
        pack_kernel,
        (
            pltpu.VMEM((pairs, order, 2 * order), p_blocks.dtype),
            pltpu.VMEM(p_blocks.shape, p_blocks.dtype),
        ),
        [VMEM], (VMEM, VMEM),
    )(*keep(p_blocks))

    order_of, parents, groups = routes(columns)
    held = {0: own}
    for key in order_of:
        held[key] = exchange(held[parents[key]], key ^ parents[key])
    pieces = []
    for group in groups:
        mine = call(
            merge_kernel, pltpu.VMEM((len(group) * pairs, order, 2 * order), own.dtype),
            [VMEM] * len(group), VMEM,
        )(*keep(*[held[key] for key in group]))
        pieces += [mine, exchange(mine, 1)]

    x = call(
        left_kernel, pltpu.VMEM((rows * entries, order, order), jnp.bfloat16),
        [VMEM, HBM], VMEM,
        [pltpu.VMEM(a_blocks.shape, a_blocks.dtype), pltpu.SemaphoreType.DMA((PARTS,))],
        limit=a_blocks.size * 4 + LIMIT,
    )(*keep(kept), pltpu.with_memory_space_constraint(a_blocks, pltpu.HBM))
    indices = (a_peer.T, a_local.T, agg_owner.T, entry_slot.T, agg_local[None])
    code = call(
        code_kernel, pltpu.SMEM((entries + 1, rows), jnp.int32), [HBM] * 5, SMEM,
        [pltpu.VMEM(array.shape, array.dtype) for array in indices]
        + [pltpu.VMEM((entries + 1, rows), jnp.int32), pltpu.SemaphoreType.DMA((5,))],
    )(*[pltpu.with_memory_space_constraint(array, pltpu.HBM) for array in indices])

    half = lanes // 2
    width = 2 * order
    acc = (2 * regions * lanes, order, width)
    most = -(-rows // regions) + 1
    visits_away = min(rows, (regions - 1) * most)
    code = pltpu.with_memory_space_constraint(code, pltpu.SMEM)
    sums, gathered = call(
        ready_kernel,
        (pltpu.VMEM(acc, jnp.float32), pltpu.VMEM((columns * pairs, order, width), p_blocks.dtype)),
        [VMEM] * 2, (VMEM, VMEM),
    )(*keep(*pieces[:2]))
    sent, sums, gathered = call(
        functools.partial(away_kernel, visits_away),
        (
            pltpu.VMEM((regions - 1, half, order, width), jnp.bfloat16),
            pltpu.VMEM(acc, jnp.float32),
            pltpu.VMEM((columns * pairs, order, width), p_blocks.dtype),
        ),
        [SMEM] + [VMEM] * (1 + len(pieces)), (VMEM, VMEM, VMEM), aliases={2: 1, 3: 2},
    )(code, *keep(x, sums, gathered, *pieces[2:]))

    received = [
        lax.ppermute(sent[n - 1], "row", [(i, (i + n) % regions) for i in range(regions)])
        for n in range(1, regions)
    ]
    own_sum = call(
        functools.partial(home_kernel, visits_away),
        pltpu.VMEM((half, order, width), jnp.float32),
        [SMEM] + [VMEM] * 3, VMEM, [pltpu.VMEM(acc, jnp.float32)],
        limit=acc[0] * order * width * 4 + LIMIT,
    )(code, *keep(x, gathered, sums))
    out = call(
        add_kernel, jax.ShapeDtypeStruct((lanes, order, order), jnp.bfloat16),
        [VMEM] * regions, VMEM, limit=4 << 20,
    )(*keep(own_sum, *received))
    return out.reshape(NC_DEV, KC, order, order)


def solution(mesh):
    in_specs = (
        P(("row", "col"), None, None, None),
        P(("row", "col"), None, None),
        P(("row", "col"), None),
        P(("row", "col"), None),
        P(("row", "col"), None),
        P(("row", "col")),
        P(("row", "col"), None),
    )
    out_specs = P(("row", "col"), None, None, None)

    return jax.shard_map(local, mesh=mesh, in_specs=in_specs, out_specs=out_specs, check_vma=False)
```

```python
import functools

import jax
import jax.numpy as jnp
from jax import lax
from jax.experimental import pallas as pl
from jax.experimental.pallas import tpu as pltpu
from jax.sharding import PartitionSpec as P

KC = 7
NC_DEV = 4
VMEM = pl.BlockSpec(memory_space=pltpu.VMEM)
SMEM = pl.BlockSpec(memory_space=pltpu.SMEM)
HBM = pl.BlockSpec(memory_space=pltpu.HBM)
LIMIT = 1 << 20
PARTS = 2


def keep(*arrays):
    return [pltpu.with_memory_space_constraint(array, pltpu.VMEM) for array in arrays]


def routes(columns):
    near = {12: 0, 2: 0, 4: 0, 10: 2, 8: 12, 14: 12, 6: 4}
    order = [key for key in near if key < columns]
    far = list(range(16, columns, 2))
    parents = {key: near[key] for key in order} | {key: key & 15 for key in far}
    groups = [[0, 2, 4, 12], [10, 8, 14], [6], far]
    groups = [[key for key in group if key < columns] for group in groups]
    return order + far, parents, [group for group in groups if group]


def slots(columns):
    keys = [key ^ core for group in routes(columns)[2] for core in range(2) for key in group]
    return {key: slot for slot, key in enumerate(keys)}


def pack_kernel(p_ref, out_ref, kept_ref):
    pairs, _, _ = out_ref.shape
    kept_ref[...] = p_ref[...]
    for j in range(pairs):
        out_ref[j] = jnp.concatenate([p_ref[j], p_ref[j + pairs]], axis=1)


def merge_kernel(*refs):
    *pieces, out_ref = refs
    start = 0
    for piece in pieces:
        out_ref[start : start + piece.shape[0]] = piece[...]
        start += piece.shape[0]


def codes(peer_ref, place_ref, owner_ref, slot_ref, row_ref):
    rows = peer_ref.shape[1]
    columns, regions = lax.axis_size("col"), lax.axis_size("row")
    pairs, lanes = rows // 2, NC_DEV * KC
    me, region = lax.axis_index("col"), lax.axis_index("row")
    key, place = peer_ref[...] ^ me, place_ref[...]
    piece = jnp.zeros_like(key)
    for value, slot in slots(columns).items():
        piece = jnp.where(key == value, slot, piece)
    high = jnp.where(place < pairs, 0, 1)
    source = piece * pairs + place - high * pairs
    relative = owner_ref[...] - region
    relative = jnp.where(relative < 0, relative + regions, relative)
    target = (relative * NC_DEV + row_ref[...]) * KC + slot_ref[...]
    return source * 65536 + target + high * (regions * lanes)


def visits(owner_ref):
    region, rows = lax.axis_index("row"), owner_ref.shape[1]
    column = lax.broadcasted_iota(jnp.int32, (rows, rows), 1)
    row = lax.broadcasted_iota(jnp.int32, (rows, rows), 0)
    away = jnp.where(owner_ref[...] != region, 1, 0) + jnp.zeros((rows, rows), jnp.int32)
    mine = jnp.sum(jnp.where(column == row, away, 0), axis=1, keepdims=True)
    before = jnp.sum(jnp.where(column < row, away, 0), axis=1, keepdims=True)
    total = jnp.sum(away, axis=1, keepdims=True)
    number = lax.broadcasted_iota(jnp.int32, (rows, 1), 0)
    place = jnp.where(mine > 0, before, total + number - before)
    return jnp.sum(jnp.where(place == column, row, 0), axis=0, keepdims=True)


def code_kernel(*refs):
    sources, (out_ref, *held, code_ref, sems) = refs[:5], refs[5:]
    copies = [
        pltpu.make_async_copy(source, target, sems.at[n])
        for n, (source, target) in enumerate(zip(sources, held))
    ]
    for copy in copies:
        copy.start()
    for copy in copies:
        copy.wait()
    entries = held[0].shape[0]
    code_ref[:entries] = codes(*held)
    code_ref[entries:] = visits(held[2])
    pltpu.sync_copy(code_ref, out_ref)


def left_kernel(p_ref, a_ref, x_ref, a_held, sems):
    rows, entries = a_ref.shape[:2]
    parts = sems.shape[0]
    step = rows // parts
    copies = []
    for n in range(parts):
        part = pl.ds(n * step, step)
        copies.append(pltpu.make_async_copy(a_ref.at[part], a_held.at[part], sems.at[n]))
        copies[n].start()
    for n in range(parts):
        copies[n].wait()
        for i in range(n * step, (n + 1) * step):
            for k in range(entries):
                x = lax.dot_general(
                    p_ref[i], a_held[i, k], (((0,), (0,)), ((), ())),
                    preferred_element_type=jnp.float32,
                )
                x_ref[i * entries + k] = x.astype(x_ref.dtype)


def fold(acc_ref, base, half, j, low):
    rows = acc_ref.shape[0] // 2
    first = jnp.where(low, acc_ref[base + j], acc_ref[rows + base + half + j])
    second = jnp.where(low, acc_ref[base + half + j], acc_ref[rows + base + j])
    order = first.shape[1] // 2
    return first + pltpu.roll(second, order, axis=1)


def accumulate(visited, code_ref, x_ref, gathered_ref, acc_ref):
    entries = code_ref.shape[0] - 1
    for i in visited:
        row = code_ref[entries, i]
        for k in range(entries):
            code = code_ref[k, row]
            source, target = code >> 16, code & 0xFFFF
            acc_ref[target] += jnp.dot(
                x_ref[row * entries + k], gathered_ref[source], preferred_element_type=jnp.float32
            )


def lower_half(order, width):
    return lax.broadcasted_iota(jnp.int32, (order, width), 1) < width // 2


def ready_kernel(*refs):
    *pieces, acc_ref, gathered_ref = refs
    acc_ref[...] = jnp.zeros_like(acc_ref)
    merge_kernel(*pieces, gathered_ref)


def away_kernel(visits, code_ref, x_ref, acc_in_ref, gathered_in_ref, *refs):
    *pieces, sent_ref, acc_ref, gathered_ref = refs
    regions, half, order, width = sent_ref.shape
    start = gathered_ref.shape[0] - sum(piece.shape[0] for piece in pieces)
    merge_kernel(*pieces, gathered_ref.at[start:])
    accumulate(range(visits), code_ref, x_ref, gathered_ref, acc_ref)
    low = lower_half(order, width)
    for n in range(regions):
        for j in range(half):
            sent_ref[n, j] = fold(acc_ref, 2 * half * (n + 1), half, j, low).astype(sent_ref.dtype)


def home_kernel(visits, code_ref, x_ref, gathered_ref, acc_in_ref, own_ref, acc_ref):
    half, order, width = own_ref.shape
    rows = code_ref.shape[1]
    total = acc_ref.shape[0] // 2
    for n in range(2):
        acc_ref[n * total : n * total + 2 * half] = acc_in_ref[n * total : n * total + 2 * half]
    accumulate(range(visits, rows), code_ref, x_ref, gathered_ref, acc_ref)
    low = lower_half(order, width)
    for j in range(half):
        own_ref[j] = fold(acc_ref, 0, half, j, low)


def add_kernel(own_ref, *refs):
    *received, out_ref = refs
    half, _, width = own_ref.shape
    for j in range(half):
        total = own_ref[j]
        for ref in received:
            total = total + ref[j].astype(jnp.float32)
        out_ref[j] = total[:, : width // 2].astype(out_ref.dtype)
        out_ref[half + j] = pltpu.roll(total, width // 2, axis=1)[:, : width // 2].astype(out_ref.dtype)


def call(kernel, out_shape, in_specs, out_specs, scratch_shapes=(), limit=LIMIT, aliases=None):
    return pl.pallas_call(
        kernel, out_shape=out_shape, in_specs=in_specs, out_specs=out_specs,
        scratch_shapes=scratch_shapes, input_output_aliases=aliases or {},
        compiler_params=pltpu.CompilerParams(vmem_limit_bytes=limit),
    )


def local(a_blocks, p_blocks, a_peer, a_local, agg_owner, agg_local, entry_slot):
    rows, entries, order, _ = a_blocks.shape
    columns, regions = lax.axis_size("col"), lax.axis_size("row")
    pairs = rows // 2
    lanes = NC_DEV * KC

    def exchange(array, bits):
        return lax.ppermute(array, "col", [(i, i ^ bits) for i in range(columns)])

    own, kept = call(
        pack_kernel,
        (
            pltpu.VMEM((pairs, order, 2 * order), p_blocks.dtype),
            pltpu.VMEM(p_blocks.shape, p_blocks.dtype),
        ),
        [VMEM], (VMEM, VMEM),
    )(*keep(p_blocks))

    order_of, parents, groups = routes(columns)
    held = {0: own}
    for key in order_of:
        held[key] = exchange(held[parents[key]], key ^ parents[key])
    pieces = []
    for group in groups:
        mine = held[group[0]]
        if len(group) > 1:
            mine = call(
                merge_kernel,
                pltpu.VMEM((len(group) * pairs, order, 2 * order), own.dtype),
                [VMEM] * len(group), VMEM,
            )(*keep(*[held[key] for key in group]))
        pieces += [mine, exchange(mine, 1)]

    x = call(
        left_kernel, pltpu.VMEM((rows * entries, order, order), jnp.bfloat16),
        [VMEM, HBM], VMEM,
        [pltpu.VMEM(a_blocks.shape, a_blocks.dtype), pltpu.SemaphoreType.DMA((PARTS,))],
        limit=a_blocks.size * 4 + LIMIT,
    )(*keep(kept), pltpu.with_memory_space_constraint(a_blocks, pltpu.HBM))
    indices = (a_peer.T, a_local.T, agg_owner.T, entry_slot.T, agg_local[None])
    code = call(
        code_kernel, pltpu.SMEM((entries + 1, rows), jnp.int32), [HBM] * 5, SMEM,
        [pltpu.VMEM(array.shape, array.dtype) for array in indices]
        + [pltpu.VMEM((entries + 1, rows), jnp.int32), pltpu.SemaphoreType.DMA((5,))],
    )(*[pltpu.with_memory_space_constraint(array, pltpu.HBM) for array in indices])

    half = lanes // 2
    width = 2 * order
    acc = (2 * regions * lanes, order, width)
    most = -(-rows // regions) + 1
    visits_away = min(rows, (regions - 1) * most)
    code = pltpu.with_memory_space_constraint(code, pltpu.SMEM)
    sums, gathered = call(
        ready_kernel,
        (pltpu.VMEM(acc, jnp.float32), pltpu.VMEM((columns * pairs, order, width), p_blocks.dtype)),
        [VMEM] * 2, (VMEM, VMEM),
    )(*keep(*pieces[:2]))
    sent, sums, gathered = call(
        functools.partial(away_kernel, visits_away),
        (
            pltpu.VMEM((regions - 1, half, order, width), jnp.bfloat16),
            pltpu.VMEM(acc, jnp.float32),
            pltpu.VMEM((columns * pairs, order, width), p_blocks.dtype),
        ),
        [SMEM] + [VMEM] * (1 + len(pieces)), (VMEM, VMEM, VMEM), aliases={2: 1, 3: 2},
    )(code, *keep(x, sums, gathered, *pieces[2:]))

    received = [
        lax.ppermute(sent[n - 1], "row", [(i, (i + n) % regions) for i in range(regions)])
        for n in range(1, regions)
    ]
    own_sum = call(
        functools.partial(home_kernel, visits_away),
        pltpu.VMEM((half, order, width), jnp.float32),
        [SMEM] + [VMEM] * 3, VMEM, [pltpu.VMEM(acc, jnp.float32)],
        limit=acc[0] * order * width * 4 + LIMIT,
    )(code, *keep(x, gathered, sums))
    out = call(
        add_kernel, jax.ShapeDtypeStruct((lanes, order, order), jnp.bfloat16),
        [VMEM] * regions, VMEM, limit=4 << 20,
    )(*keep(own_sum, *received))
    return out.reshape(NC_DEV, KC, order, order)


def solution(mesh):
    in_specs = (
        P(("row", "col"), None, None, None),
        P(("row", "col"), None, None),
        P(("row", "col"), None),
        P(("row", "col"), None),
        P(("row", "col"), None),
        P(("row", "col")),
        P(("row", "col"), None),
    )
    out_specs = P(("row", "col"), None, None, None)

    return jax.shard_map(local, mesh=mesh, in_specs=in_specs, out_specs=out_specs, check_vma=False)
```

```python
import functools

import jax
import jax.numpy as jnp
from jax import lax
from jax.experimental import pallas as pl
from jax.experimental.pallas import tpu as pltpu
from jax.sharding import PartitionSpec as P

KC = 7
NC_DEV = 4
VMEM = pl.BlockSpec(memory_space=pltpu.VMEM)
SMEM = pl.BlockSpec(memory_space=pltpu.SMEM)
HBM = pl.BlockSpec(memory_space=pltpu.HBM)
LIMIT = 1 << 20
PARTS = 1


def keep(*arrays):
    return [pltpu.with_memory_space_constraint(array, pltpu.VMEM) for array in arrays]


def routes(columns):
    near = {12: 0, 2: 0, 4: 0, 10: 2, 8: 12, 14: 12, 6: 4}
    order = [key for key in near if key < columns]
    far = list(range(16, columns, 2))
    parents = {key: near[key] for key in order} | {key: key & 15 for key in far}
    groups = [[0, 2, 4, 12], [10, 8, 14], [6], far]
    groups = [[key for key in group if key < columns] for group in groups]
    return order + far, parents, [group for group in groups if group]


def slots(columns):
    keys = [key ^ core for group in routes(columns)[2] for core in range(2) for key in group]
    return {key: slot for slot, key in enumerate(keys)}


def pack_kernel(p_ref, out_ref, kept_ref):
    pairs, _, _ = out_ref.shape
    kept_ref[...] = p_ref[...]
    for j in range(pairs):
        out_ref[j] = jnp.concatenate([p_ref[j], p_ref[j + pairs]], axis=1)


def merge_kernel(*refs):
    *pieces, out_ref = refs
    start = 0
    for piece in pieces:
        out_ref[start : start + piece.shape[0]] = piece[...]
        start += piece.shape[0]


def codes(peer_ref, place_ref, owner_ref, slot_ref, row_ref):
    rows = peer_ref.shape[1]
    columns, regions = lax.axis_size("col"), lax.axis_size("row")
    pairs, lanes = rows // 2, NC_DEV * KC
    me, region = lax.axis_index("col"), lax.axis_index("row")
    key, place = peer_ref[...] ^ me, place_ref[...]
    piece = jnp.zeros_like(key)
    for value, slot in slots(columns).items():
        piece = jnp.where(key == value, slot, piece)
    high = jnp.where(place < pairs, 0, 1)
    source = piece * pairs + place - high * pairs
    relative = owner_ref[...] - region
    relative = jnp.where(relative < 0, relative + regions, relative)
    target = (relative * NC_DEV + row_ref[...]) * KC + slot_ref[...]
    return source * 65536 + target + high * (regions * lanes)


def visits(owner_ref):
    region, rows = lax.axis_index("row"), owner_ref.shape[1]
    column = lax.broadcasted_iota(jnp.int32, (rows, rows), 1)
    row = lax.broadcasted_iota(jnp.int32, (rows, rows), 0)
    away = jnp.where(owner_ref[...] != region, 1, 0) + jnp.zeros((rows, rows), jnp.int32)
    mine = jnp.sum(jnp.where(column == row, away, 0), axis=1, keepdims=True)
    before = jnp.sum(jnp.where(column < row, away, 0), axis=1, keepdims=True)
    total = jnp.sum(away, axis=1, keepdims=True)
    number = lax.broadcasted_iota(jnp.int32, (rows, 1), 0)
    place = jnp.where(mine > 0, before, total + number - before)
    return jnp.sum(jnp.where(place == column, row, 0), axis=0, keepdims=True)


def code_kernel(*refs):
    sources, (out_ref, *held, code_ref, sems) = refs[:5], refs[5:]
    copies = [
        pltpu.make_async_copy(source, target, sems.at[n])
        for n, (source, target) in enumerate(zip(sources, held))
    ]
    for copy in copies:
        copy.start()
    for copy in copies:
        copy.wait()
    entries = held[0].shape[0]
    code_ref[:entries] = codes(*held)
    code_ref[entries:] = visits(held[2])
    pltpu.sync_copy(code_ref, out_ref)


def left_kernel(p_ref, a_ref, x_ref, a_held, sems):
    rows, entries = a_ref.shape[:2]
    parts = sems.shape[0]
    step = rows // parts
    copies = []
    for n in range(parts):
        part = pl.ds(n * step, step)
        copies.append(pltpu.make_async_copy(a_ref.at[part], a_held.at[part], sems.at[n]))
        copies[n].start()
    for n in range(parts):
        copies[n].wait()
        for i in range(n * step, (n + 1) * step):
            for k in range(entries):
                x = lax.dot_general(
                    p_ref[i], a_held[i, k], (((0,), (0,)), ((), ())),
                    preferred_element_type=jnp.float32,
                )
                x_ref[i * entries + k] = x.astype(x_ref.dtype)


def fold(acc_ref, base, half, j, low):
    rows = acc_ref.shape[0] // 2
    first = jnp.where(low, acc_ref[base + j], acc_ref[rows + base + half + j])
    second = jnp.where(low, acc_ref[base + half + j], acc_ref[rows + base + j])
    order = first.shape[1] // 2
    return first + pltpu.roll(second, order, axis=1)


def accumulate(visited, code_ref, x_ref, gathered_ref, acc_ref):
    entries = code_ref.shape[0] - 1
    for i in visited:
        row = code_ref[entries, i]
        for k in range(entries):
            code = code_ref[k, row]
            source, target = code >> 16, code & 0xFFFF
            acc_ref[target] += jnp.dot(
                x_ref[row * entries + k], gathered_ref[source], preferred_element_type=jnp.float32
            )


def lower_half(order, width):
    return lax.broadcasted_iota(jnp.int32, (order, width), 1) < width // 2


def place(starts, pieces, gathered_ref):
    for start, piece in zip(starts, pieces):
        gathered_ref[start : start + piece.shape[0]] = piece[...]


def ready_kernel(starts, *refs):
    *pieces, acc_ref, gathered_ref = refs
    acc_ref[...] = jnp.zeros_like(acc_ref)
    place(starts, pieces, gathered_ref)


def away_kernel(visits, starts, code_ref, x_ref, acc_in_ref, gathered_in_ref, *refs):
    *pieces, sent_ref, acc_ref, gathered_ref = refs
    regions, half, order, width = sent_ref.shape
    place(starts, pieces, gathered_ref)
    accumulate(range(visits), code_ref, x_ref, gathered_ref, acc_ref)
    low = lower_half(order, width)
    for n in range(regions):
        for j in range(half):
            sent_ref[n, j] = fold(acc_ref, 2 * half * (n + 1), half, j, low).astype(sent_ref.dtype)


def home_kernel(visits, code_ref, x_ref, gathered_ref, acc_in_ref, own_ref, acc_ref):
    half, order, width = own_ref.shape
    rows = code_ref.shape[1]
    total = acc_ref.shape[0] // 2
    for n in range(2):
        acc_ref[n * total : n * total + 2 * half] = acc_in_ref[n * total : n * total + 2 * half]
    accumulate(range(visits, rows), code_ref, x_ref, gathered_ref, acc_ref)
    low = lower_half(order, width)
    for j in range(half):
        own_ref[j] = fold(acc_ref, 0, half, j, low)


def add_kernel(own_ref, *refs):
    *received, out_ref = refs
    half, _, width = own_ref.shape
    for j in range(half):
        total = own_ref[j]
        for ref in received:
            total = total + ref[j].astype(jnp.float32)
        out_ref[j] = total[:, : width // 2].astype(out_ref.dtype)
        out_ref[half + j] = pltpu.roll(total, width // 2, axis=1)[:, : width // 2].astype(out_ref.dtype)


def call(kernel, out_shape, in_specs, out_specs, scratch_shapes=(), limit=LIMIT, aliases=None):
    return pl.pallas_call(
        kernel, out_shape=out_shape, in_specs=in_specs, out_specs=out_specs,
        scratch_shapes=scratch_shapes, input_output_aliases=aliases or {},
        compiler_params=pltpu.CompilerParams(vmem_limit_bytes=limit),
    )


def local(a_blocks, p_blocks, a_peer, a_local, agg_owner, agg_local, entry_slot):
    rows, entries, order, _ = a_blocks.shape
    columns, regions = lax.axis_size("col"), lax.axis_size("row")
    pairs = rows // 2
    lanes = NC_DEV * KC

    def exchange(array, bits):
        return lax.ppermute(array, "col", [(i, i ^ bits) for i in range(columns)])

    own, kept = call(
        pack_kernel,
        (
            pltpu.VMEM((pairs, order, 2 * order), p_blocks.dtype),
            pltpu.VMEM(p_blocks.shape, p_blocks.dtype),
        ),
        [VMEM], (VMEM, VMEM),
    )(*keep(p_blocks))

    order_of, parents, groups = routes(columns)
    held = {0: own}
    for key in order_of:
        held[key] = exchange(held[parents[key]], key ^ parents[key])
    pieces = []
    for group in groups:
        mine = held[group[0]]
        if len(group) > 1:
            mine = call(
                merge_kernel,
                pltpu.VMEM((len(group) * pairs, order, 2 * order), own.dtype),
                [VMEM] * len(group), VMEM,
            )(*keep(*[held[key] for key in group]))
        pieces += [mine, exchange(mine, 1)]

    x = call(
        left_kernel, pltpu.VMEM((rows * entries, order, order), jnp.bfloat16),
        [VMEM, HBM], VMEM,
        [pltpu.VMEM(a_blocks.shape, a_blocks.dtype), pltpu.SemaphoreType.DMA((PARTS,))],
        limit=a_blocks.size * 4 + LIMIT,
    )(*keep(kept), pltpu.with_memory_space_constraint(a_blocks, pltpu.HBM))
    indices = (a_peer.T, a_local.T, agg_owner.T, entry_slot.T, agg_local[None])
    code = call(
        code_kernel, pltpu.SMEM((entries + 1, rows), jnp.int32), [HBM] * 5, SMEM,
        [pltpu.VMEM(array.shape, array.dtype) for array in indices]
        + [pltpu.VMEM((entries + 1, rows), jnp.int32), pltpu.SemaphoreType.DMA((5,))],
    )(*[pltpu.with_memory_space_constraint(array, pltpu.HBM) for array in indices])

    half = lanes // 2
    width = 2 * order
    acc = (2 * regions * lanes, order, width)
    most = -(-rows // regions) + 1
    visits_away = min(rows, (regions - 1) * most)
    code = pltpu.with_memory_space_constraint(code, pltpu.SMEM)
    starts = [sum(piece.shape[0] for piece in pieces[:n]) for n in range(len(pieces))]
    late = [n for n in range(3, len(pieces), 2)]
    soon = [n for n in range(len(pieces)) if n not in late]
    sums, gathered = call(
        functools.partial(ready_kernel, [starts[n] for n in soon]),
        (pltpu.VMEM(acc, jnp.float32), pltpu.VMEM((columns * pairs, order, width), p_blocks.dtype)),
        [VMEM] * len(soon), (VMEM, VMEM),
    )(*keep(*[pieces[n] for n in soon]))
    sent, sums, gathered = call(
        functools.partial(away_kernel, visits_away, [starts[n] for n in late]),
        (
            pltpu.VMEM((regions - 1, half, order, width), jnp.bfloat16),
            pltpu.VMEM(acc, jnp.float32),
            pltpu.VMEM((columns * pairs, order, width), p_blocks.dtype),
        ),
        [SMEM] + [VMEM] * (3 + len(late)), (VMEM, VMEM, VMEM), aliases={2: 1, 3: 2},
    )(code, *keep(x, sums, gathered, *[pieces[n] for n in late]))

    received = [
        lax.ppermute(sent[n - 1], "row", [(i, (i + n) % regions) for i in range(regions)])
        for n in range(1, regions)
    ]
    own_sum = call(
        functools.partial(home_kernel, visits_away),
        pltpu.VMEM((half, order, width), jnp.float32),
        [SMEM] + [VMEM] * 3, VMEM, [pltpu.VMEM(acc, jnp.float32)],
        limit=acc[0] * order * width * 4 + LIMIT,
    )(code, *keep(x, gathered, sums))
    out = call(
        add_kernel, jax.ShapeDtypeStruct((lanes, order, order), jnp.bfloat16),
        [VMEM] * regions, VMEM, limit=4 << 20,
    )(*keep(own_sum, *received))
    return out.reshape(NC_DEV, KC, order, order)


def solution(mesh):
    in_specs = (
        P(("row", "col"), None, None, None),
        P(("row", "col"), None, None),
        P(("row", "col"), None),
        P(("row", "col"), None),
        P(("row", "col"), None),
        P(("row", "col")),
        P(("row", "col"), None),
    )
    out_specs = P(("row", "col"), None, None, None)

    return jax.shard_map(local, mesh=mesh, in_specs=in_specs, out_specs=out_specs, check_vma=False)
```
